1024 devices in a mesh: gx: 4 (over x), gy: 8 (over y, core), gz: 32 (over z).
Axes of the slice: x: 4, y: 4, z: 32, core: 2. Of those that a mesh axis runs over, the one named last changes fastest.
Arguments:
- residual_in: float32 [4, 8, 32, 128, 768], P('gx', 'gy', 'gz'), as said below
- schur: float32 [4, 8, 32, 768, 768], P('gx', 'gy', 'gz'), as said below
- modes: float32 [4, 8, 32, 6, 768], P('gx', 'gy', 'gz'), may hold values from -0.875 to 0.875
- coarse_inv: float32 [4, 8, 192, 192], P('gx', 'gy', 'gz'), as said below
Outputs:
- multipliers: float32 [4, 8, 32, 128, 768], P('gx', 'gy', 'gz')
- residual: float32 [4, 8, 32, 128, 768], P('gx', 'gy', 'gz')
The draws below stay inside these ranges and needn't reach their ends.
Inputs may be any that keep to these rules, and one draw needn't show every extreme that they name: `residual_in`: each multiplier has the same value on both sides of its face. `schur`: every subdomain's matrix is symmetric positive definite. `coarse_inv`: every coarse block is symmetric positive definite.
All inputs are finite; a program needn't handle non-finite values.
Results may differ from the reference program's by a relative error of at most 0.0003.
Values sent between devices are 32-bit elements; how exact they have to be, the bound alone decides.
A program may use at most 32 MiB of HBM per device.

```python
import jax
import jax.numpy as jnp
from jax import lax

FACE = 128
IF = 768
LOADS = 128
MODES = 6
ITERS = 4
CN = 192
N_GX = 4
N_GY = 8
N_GZ = 32


def draw_residual_in(key, part):
    shape = (N_GX, N_GY, N_GZ, 3, LOADS, FACE)
    base = jax.random.normal(key, shape, jnp.float32)
    face_x = base[:, :, :, 0]
    face_y = base[:, :, :, 1]
    face_z = base[:, :, :, 2]
    pieces = [face_x, jnp.roll(face_x, -1, axis=0), face_y, jnp.roll(face_y, -1, axis=1), face_z, jnp.roll(face_z, -1, axis=2)]
    return jnp.concatenate(pieces, axis=-1)


def draw_schur(key, part):
    key_diag = jax.random.fold_in(key, 11)
    key_off = jax.random.fold_in(key, 12)
    diag = jnp.exp(jax.random.uniform(key_diag, (N_GX, N_GY, N_GZ, IF), jnp.float32, jnp.log(2.0), jnp.log(5.0)))
    shape = (N_GX, N_GY, N_GZ, IF, IF)
    noise = jax.random.normal(key_off, shape, jnp.float32)
    noise = noise * IF ** (-0.5)
    sym = 0.5 * (noise + jnp.swapaxes(noise, -1, -2))
    return sym + diag[..., None] * jnp.eye(IF, dtype=jnp.float32)


def draw_coarse_inv(key, part):
    key_diag = jax.random.fold_in(key, 21)
    key_off = jax.random.fold_in(key, 22)
    diag = jnp.exp(jax.random.uniform(key_diag, (N_GX, N_GY, CN), jnp.float32, jnp.log(1.5), jnp.log(4.0)))
    shape = (N_GX, N_GY, CN, CN)
    noise = jax.random.normal(key_off, shape, jnp.float32)
    noise = noise * (0.7 * CN ** (-0.5))
    sym = 0.5 * (noise + jnp.swapaxes(noise, -1, -2))
    return sym + diag[..., None] * jnp.eye(CN, dtype=jnp.float32)


def shard_levels(key, shape, shards, least, high):
    factor_of, own = 1.0, jax.random.fold_in(key, 6)
    for axis_at, shards_of in shards:
        heights = jnp.exp(jax.random.uniform(jax.random.fold_in(own, axis_at), (shards_of,), jnp.float32, least / len(shards), high / len(shards)))
        factor_of = factor_of * jnp.repeat(heights, shape[axis_at] // shards_of).reshape([-1 if axis == axis_at else 1 for axis in range(len(shape))])
    return factor_of


def bell_draw(own_key, shape, deviation, bound, shards=(), kind=jnp.bfloat16):
    factor_of = shard_levels(own_key, shape, shards, -0.22, 0.18) if shards else 1.0
    drawn = jax.random.normal(own_key, shape, jnp.float32) * deviation * factor_of
    return jnp.minimum(jnp.maximum(drawn, -bound), bound).astype(kind)


def setup_inputs(seed: int = 0) -> dict:
    key_of = jax.random.split(jax.random.key(seed), 5)
    residual_in = draw_residual_in(jax.random.fold_in(key_of[4], 71), 0)
    schur = draw_schur(jax.random.fold_in(key_of[4], 71), 0)
    modes = bell_draw(key_of[2], (N_GX, N_GY, N_GZ, MODES, IF), (IF // 16) ** -0.5, 0.875, ((0, 4), (1, 8), (2, 32)), jnp.float32)
    coarse_inv = draw_coarse_inv(jax.random.fold_in(key_of[4], 71), 0)
    return dict(residual_in=residual_in, schur=schur, modes=modes, coarse_inv=coarse_inv)


def face_signs(face):
    return jnp.repeat(jnp.array([1.0, -1.0, 1.0, -1.0, 1.0, -1.0], dtype=jnp.float32), face)


def subdomain_product(pair):
    matrix, vector = pair
    return jnp.einsum('rj,ij->ri', vector, matrix, precision=lax.Precision.HIGHEST)


def assemble(values):
    parts = []
    for axis_id in range(3):
        low_face = values[..., 2 * axis_id * FACE:(2 * axis_id + 1) * FACE]
        high_face = values[..., (2 * axis_id + 1) * FACE:(2 * axis_id + 2) * FACE]
        from_low = jnp.roll(high_face, 1, axis=axis_id)
        from_high = jnp.roll(low_face, -1, axis=axis_id)
        parts.append(low_face - from_low)
        parts.append(from_high - high_face)
    return jnp.concatenate(parts, axis=-1)


def operate(field, schur, modes, coarse_inv):
    sign = face_signs(FACE)
    u = sign * field
    shape = u.shape
    flat_schur = schur.reshape(-1, IF, IF)
    flat_u = u.reshape(-1, LOADS, IF)
    local = lax.map(subdomain_product, (flat_schur, flat_u)).reshape(shape)
    loads = jnp.einsum('xyzmj,xyzrj->xyzmr', modes, u, precision=lax.Precision.HIGHEST)
    column = loads.reshape(N_GX, N_GY, CN, LOADS)
    amp = jnp.einsum('xyab,xybr->xyar', coarse_inv, column, precision=lax.Precision.HIGHEST)
    amp = amp.reshape(N_GX, N_GY, N_GZ, MODES, LOADS)
    coarse_term = jnp.einsum('xyzmr,xyzmj->xyzrj', amp, modes, precision=lax.Precision.HIGHEST)
    return assemble(local + coarse_term)


def inner_dot(left, right):
    return 0.5 * jnp.sum(left * right, axis=(0, 1, 2, 4))


def reference(residual_in, schur, modes, coarse_inv):
    resid = residual_in
    mult = jnp.zeros_like(residual_in)
    image = operate(resid, schur, modes, coarse_inv)
    norm_now = inner_dot(resid, resid)
    alpha = norm_now / inner_dot(resid, image)
    direction = resid
    along = image
    for step in range(ITERS):
        mult = mult + alpha[:, None] * direction
        resid = resid - alpha[:, None] * along
        if step + 1 < ITERS:
            image = operate(resid, schur, modes, coarse_inv)
            norm_next = inner_dot(resid, resid)
            curv = inner_dot(resid, image)
            ratio = norm_next / norm_now
            alpha = norm_next / (curv - ratio * norm_next / alpha)
            direction = resid + ratio[:, None] * direction
            along = image + ratio[:, None] * along
            norm_now = norm_next
    return mult, resid
```

```python
import functools

import jax
import jax.numpy as jnp
from jax import lax
from jax.experimental import pallas as pl
from jax.experimental.pallas import tpu as pltpu
from jax.sharding import PartitionSpec as P

MESH = pl.DeviceIdType.MESH
ITERS = 4
FACE = 128
IF = 6 * FACE
LOADS = 128
MODES = 6
SLOT = 8
AUG = IF + 16
F32 = jnp.float32
BF16 = jnp.bfloat16


def gather_plan(nz):
    if nz == 32:
        direct = [13, -13, 7, -7, 3, -3, 2, -2, 1, -1]
        relays = [
            (7, [3, -3, 2, -2, 1, -1]),
            (-7, [-3, 3, -2, 2, -1, 1]),
            (13, [3, -2, 2, -1, 1]),
            (-13, [-2, 2, -1, 1]),
        ]
        return direct, relays
    direct = [1]
    relays = [(1, list(range(1, nz - 1)))]
    return direct, relays


def split(x):
    hi = x.astype(BF16)
    return hi, (x - hi.astype(F32)).astype(BF16)


def mm(a, b):
    return jnp.dot(a, b, preferred_element_type=F32)


def kernel(
    sizes, res_hbm, schur_hbm, modes_hbm, coarse_hbm, mult_ref, out_ref,
    res_v, schur_v, modes_v, coarse_v, modes8, coarse8, cbuf, c_hi, c_lo, pmodes, tcat, m_hi, m_lo, ucat,
    r_buf, p_buf, s_buf, x_buf, y_buf, q_buf, zq_buf, zs_buf,
    gbuf, abuf, acol, xysrc, xybuf, hbuf,
    local_sem, schur_sem, c_send, c_recv, m_send, m_recv, z_send, z_recv, h_send, h_recv, a_send, a_recv, xy_send, xy_recv,
):
    nx, ny, nz = sizes
    mx, my, mz = lax.axis_index("gx"), lax.axis_index("gy"), lax.axis_index("gz")

    def device(dx, dy, dz):
        return (lax.rem(mx + dx % nx, nx), lax.rem(my + dy % ny, ny), lax.rem(mz + dz % nz, nz))

    direct, relays = gather_plan(nz)
    others = [(dx, dy) for dx in range(nx) for dy in range(ny) if dx or dy]

    def far(d):
        dx, dy = d
        return -(min(dx, nx - dx) + min(dy, ny - dy))

    others.sort(key=far)
    faces = [(-1, 0, 0), (1, 0, 0), (0, -1, 0), (0, 1, 0), (0, 0, -1), (0, 0, 1)]

    load_modes = pltpu.make_async_copy(modes_hbm, modes_v, local_sem.at[0])
    load_coarse = pltpu.make_async_copy(coarse_hbm, coarse_v, local_sem.at[1])
    load_res = pltpu.make_async_copy(res_hbm, res_v, local_sem.at[2])
    load_modes.start()
    load_coarse.start()
    load_res.start()
    load_schur = []
    for f in range(6):
        rows = pl.ds(f * FACE, FACE)
        copy = pltpu.make_async_copy(schur_hbm.at[rows], schur_v.at[rows], schur_sem.at[f])
        copy.start()
        load_schur.append(copy)

    barrier = pltpu.get_barrier_semaphore()
    z_targets = sorted(set(o % nz for o in direct) | set(o % nz for _, steps in relays for o in steps))
    z_all = sorted(set(z_targets) | set((-o) % nz for o in z_targets) | {1, nz - 1})
    for dz in z_all:
        pl.semaphore_signal(barrier, inc=1, device_id=device(0, 0, dz), device_id_type=MESH)
    for dx, dy in others:
        pl.semaphore_signal(barrier, inc=1, device_id=device(dx, dy, 0), device_id_type=MESH)

    coarse8[...] = jnp.zeros_like(coarse8)
    modes8[...] = jnp.zeros_like(modes8)
    load_coarse.wait()
    coarse8[0:MODES] = coarse_v[...]
    cn = MODES * nz
    cp = SLOT * nz
    row = lax.broadcasted_iota(jnp.int32, (cn, cp), 0)
    col = lax.broadcasted_iota(jnp.int32, (cn, cp), 1)
    mode = lax.rem(col, SLOT)
    pick = (row == MODES * (col // SLOT) + mode) & (mode < MODES)
    spread = jnp.where(pick, 1.0, 0.0).astype(F32)
    cbuf[mz] = jnp.dot(coarse8[...], spread, precision=lax.Precision.HIGHEST, preferred_element_type=F32)
    load_modes.wait()
    modes8[0:MODES] = modes_v[...]

    def z_copy(buf, send, recv, n, source, step, offset):
        slot = lax.rem(mz + (-source) % nz, nz)
        return pltpu.make_async_remote_copy(
            src_ref=buf.at[slot], dst_ref=buf.at[slot], send_sem=send.at[n], recv_sem=recv.at[offset % nz],
            device_id=device(0, 0, step), device_id_type=MESH,
        )

    def z_arrival(buf, send, recv, offset):
        slot = lax.rem(mz + (-offset) % nz, nz)
        return pltpu.make_async_remote_copy(
            src_ref=buf.at[slot], dst_ref=buf.at[slot], send_sem=send.at[0], recv_sem=recv.at[offset % nz],
            device_id=device(0, 0, 1), device_id_type=MESH,
        )

    def z_first(buf, send, recv):
        return [z_copy(buf, send, recv, n, 0, o, o) for n, o in enumerate(direct)]

    def z_relays(buf, send, recv):
        n, out = len(direct), []
        for centre, steps in relays:
            copies = []
            for step in steps:
                copies.append(z_copy(buf, send, recv, n, centre, step, centre + step))
                n += 1
            out.append((centre, copies))
        return out

    relayed = [centre % nz for centre, _ in relays]
    rest = [o for o in range(1, nz) if o not in relayed]

    def relay(buf, send, recv):
        for centre, copies in z_relays(buf, send, recv):
            z_arrival(buf, send, recv, centre).wait_recv()
            for copy in copies:
                copy.start()

    def finish(buf, send, recv):
        for offset in rest:
            z_arrival(buf, send, recv, offset).wait_recv()

    def sent(buf, send, recv):
        for copy in z_first(buf, send, recv):
            copy.wait_send()
        for _, copies in z_relays(buf, send, recv):
            for copy in copies:
                copy.wait_send()

    pl.semaphore_wait(barrier, len(z_all) + len(others))

    for copy in z_first(cbuf, c_send, c_recv):
        copy.start()

    def mode_copy(f):
        return pltpu.make_async_remote_copy(
            src_ref=modes8.at[:, pl.ds(f * FACE, FACE)], dst_ref=pmodes.at[f ^ 1], send_sem=m_send.at[f], recv_sem=m_recv.at[f ^ 1],
            device_id=device(*faces[f]), device_id_type=MESH,
        )

    for f in range(6):
        mode_copy(f).start()

    def halo_copy(par, f):
        return pltpu.make_async_remote_copy(
            src_ref=y_buf.at[pl.ds(f * FACE, FACE)], dst_ref=hbuf.at[par, f ^ 1], send_sem=h_send.at[f], recv_sem=h_recv.at[par, f ^ 1],
            device_id=device(*faces[f]), device_id_type=MESH,
        )

    def halo_arrival(par, f):
        return pltpu.make_async_remote_copy(
            src_ref=y_buf.at[pl.ds(f * FACE, FACE)], dst_ref=hbuf.at[par, f], send_sem=h_send.at[f], recv_sem=h_recv.at[par, f],
            device_id=device(*faces[f]), device_id_type=MESH,
        )

    def a_copy(par, f):
        return pltpu.make_async_remote_copy(
            src_ref=acol.at[mz], dst_ref=abuf.at[par, f ^ 1], send_sem=a_send.at[f], recv_sem=a_recv.at[par, f ^ 1],
            device_id=device(*faces[f]), device_id_type=MESH,
        )

    def a_arrival(par, f):
        return pltpu.make_async_remote_copy(
            src_ref=acol.at[mz], dst_ref=abuf.at[par, f], send_sem=a_send.at[f], recv_sem=a_recv.at[par, f],
            device_id=device(*faces[f]), device_id_type=MESH,
        )

    my_slot = mx * ny + my

    def xy_copy(par, n):
        dx, dy = others[n]
        return pltpu.make_async_remote_copy(
            src_ref=xysrc, dst_ref=xybuf.at[par, my_slot], send_sem=xy_send.at[n], recv_sem=xy_recv.at[par, n],
            device_id=device(dx, dy, 0), device_id_type=MESH,
        )

    def xy_arrival(par, n):
        dx, dy = others[n]
        from_x, from_y, _ = device(-dx, -dy, 0)
        return pltpu.make_async_remote_copy(
            src_ref=xysrc, dst_ref=xybuf.at[par, from_x * ny + from_y], send_sem=xy_send.at[n], recv_sem=xy_recv.at[par, n],
            device_id=device(dx, dy, 0), device_id_type=MESH,
        )

    def apply_local():
        for lo, size in ((0, 400), (400, 384)):
            rows = slice(lo, lo + size)
            both = mm(m_hi[rows], ucat[...])
            zq_buf[rows] = both[:, :LOADS] + both[:, LOADS:] + mm(m_lo[rows], ucat[:, :LOADS])

    load_res.wait()
    for f in range(6):
        block = jnp.transpose(res_v[:, f * FACE:(f + 1) * FACE])
        if f % 2:
            block = -block
        rows = slice(f * FACE, (f + 1) * FACE)
        r_buf[0, rows] = block
        hi, lo = split(block)
        ucat[rows, :LOADS] = hi
        ucat[rows, LOADS:] = lo
    w_aug = jnp.concatenate([modes8[...], jnp.zeros((8, IF), F32)], axis=0)
    hi, lo = split(w_aug)
    m_hi[IF:AUG] = hi
    m_lo[IF:AUG] = lo
    for f in range(6):
        load_schur[f].wait()
        rows = slice(f * FACE, (f + 1) * FACE)
        hi, lo = split(schur_v[rows])
        m_hi[rows] = hi
        m_lo[rows] = lo
    apply_local()

    def post(par, r_par, first, alpha):
        norm = jnp.zeros((8, LOADS), F32)
        energy = jnp.zeros((8, LOADS), F32)
        for f in range(6):
            rows = slice(f * FACE, (f + 1) * FACE)
            y = zq_buf[rows] if first else y_buf[rows] - alpha * zs_buf[rows]
            y_buf[rows] = y
            r = r_buf[r_par, rows]
            norm = norm + jnp.sum((r * r).reshape(FACE // 8, 8, LOADS), axis=0)
            energy = energy + jnp.sum((r * y).reshape(FACE // 8, 8, LOADS), axis=0)
        rows = slice(IF, IF + SLOT)
        g = zq_buf[rows] if first else y_buf[rows] - alpha * zs_buf[rows]
        y_buf[rows] = g
        gbuf[par, mz] = g
        gbuf[par, mz, MODES:MODES + 1] = jnp.sum(norm, axis=0, keepdims=True)
        gbuf[par, mz, MODES + 1:SLOT] = jnp.sum(energy, axis=0, keepdims=True)

    def launch(par):
        for copy in z_first(gbuf.at[par], z_send, z_recv.at[par]):
            copy.start()
        for f in (4, 5, 0, 1, 2, 3):
            halo_copy(par, f).start()

    post(0, 0, True, None)
    launch(0)

    x_buf[...] = jnp.zeros_like(x_buf)
    p_buf[...] = jnp.zeros_like(p_buf)
    s_buf[...] = jnp.zeros_like(s_buf)
    zs_buf[...] = jnp.zeros_like(zs_buf)
    relay(cbuf, c_send, c_recv)

    for f in range(6):
        mode_copy(f).wait_send()
    for f in range(6):
        pltpu.make_async_remote_copy(
            src_ref=modes8.at[:, pl.ds(f * FACE, FACE)], dst_ref=pmodes.at[f], send_sem=m_send.at[f], recv_sem=m_recv.at[f],
            device_id=device(*faces[f]), device_id_type=MESH,
        ).wait_recv()
    zero8 = jnp.zeros((SLOT, FACE), F32)
    for f in range(6):
        pieces = [zero8] * 8
        pieces[0] = modes8[:, f * FACE:(f + 1) * FACE]
        pieces[1 + f] = -pmodes[f]
        hi, lo = split(jnp.concatenate(pieces, axis=0))
        stack = jnp.concatenate([hi.astype(F32), lo.astype(F32), hi.astype(F32), jnp.zeros((64, FACE), F32)], axis=0)
        tcat[f * FACE:(f + 1) * FACE] = jnp.transpose(stack).astype(BF16)

    def step(k, carry):
        alpha_before, rr = carry
        par = lax.rem(k, 2)
        after = 1 - par
        g_now, recv_now = gbuf.at[par], z_recv.at[par]
        relay(g_now, z_send, recv_now)

        @pl.when(k == 0)
        def _():
            finish(cbuf, c_send, c_recv)
            hi, lo = split(cbuf[...].reshape(cp, cp))
            c_hi[...] = hi
            c_lo[...] = lo
            sent(cbuf, c_send, c_recv)

        finish(g_now, z_send, recv_now)
        g = gbuf[par]
        total = jnp.sum(g, axis=0)
        g = g.reshape(cp, LOADS)
        g_hi, g_lo = split(g)
        both = mm(c_hi[...], jnp.concatenate([g_hi, g_lo], axis=1))
        a = both[:, :LOADS] + both[:, LOADS:] + mm(c_lo[...], g_hi)
        acol[...] = a.reshape(nz, SLOT, LOADS)
        for f in range(4):
            a_copy(par, f).start()
        coarse_energy = jnp.sum(a * g, axis=0, keepdims=True)
        xysrc[0:1] = total[MODES:MODES + 1]
        xysrc[1:2] = total[MODES + 1:SLOT] + coarse_energy
        for n in range(len(others)):
            xy_copy(par, n).start()
        xybuf[par, my_slot] = xysrc[...]

        for f in range(6):
            halo_arrival(par, f).wait_recv()
        for f in range(4):
            a_arrival(par, f).wait_recv()
        pieces = [acol[mz]] + [abuf[par, f] for f in range(4)]
        pieces += [acol[lax.rem(mz + nz - 1, nz)], acol[lax.rem(mz + 1, nz)], jnp.zeros((SLOT, LOADS), F32)]
        hi, lo = split(jnp.concatenate(pieces, axis=0))
        amps = jnp.concatenate([hi, hi, lo, jnp.zeros((64, LOADS), BF16)], axis=0)
        for f in range(6):
            rows = slice(f * FACE, (f + 1) * FACE)
            q = y_buf[rows] - hbuf[par, f] + mm(tcat[rows], amps)
            q_buf[rows] = q
            hi, lo = split(q)
            ucat[rows, :LOADS] = hi
            ucat[rows, LOADS:] = lo

        @pl.when(k < ITERS - 1)
        def _():
            apply_local()

        sent(g_now, z_send, recv_now)
        for f in range(6):
            halo_copy(par, f).wait_send()
        for f in range(4):
            a_copy(par, f).wait_send()
        for n in range(len(others)):
            xy_copy(par, n).wait_send()
        for n in range(len(others)):
            xy_arrival(par, n).wait_recv()
        sums = jnp.sum(xybuf[par], axis=0)
        new = 0.5 * sums[0:1]
        curv = sums[1:2]
        beta = jnp.where(k == 0, jnp.zeros_like(new), new / rr)
        alpha = new / (curv - beta * new / alpha_before)

        for f in range(6):
            rows = slice(f * FACE, (f + 1) * FACE)
            s = q_buf[rows] + beta * s_buf[rows]
            s_buf[rows] = s
            r_buf[after, rows] = r_buf[par, rows] - alpha * s

        @pl.when(k < ITERS - 1)
        def _():
            for f in range(6):
                rows = slice(f * FACE, (f + 1) * FACE)
                zs_buf[rows] = zq_buf[rows] + beta * zs_buf[rows]
            rows = slice(IF, IF + SLOT)
            zs_buf[rows] = zq_buf[rows] + beta * zs_buf[rows]
            post(after, after, False, alpha)
            launch(after)

        for f in range(6):
            rows = slice(f * FACE, (f + 1) * FACE)
            p = r_buf[par, rows] + beta * p_buf[rows]
            p_buf[rows] = p
            x_buf[rows] = x_buf[rows] + alpha * p
        return alpha, new

    one = jnp.ones((1, LOADS), F32)
    lax.fori_loop(0, ITERS, step, (one, one))

    for f in range(6):
        rows = slice(f * FACE, (f + 1) * FACE)
        x = jnp.transpose(x_buf[rows])
        r = jnp.transpose(r_buf[ITERS % 2, rows])
        mult_ref[:, rows] = -x if f % 2 else x
        out_ref[:, rows] = -r if f % 2 else r


def body(sizes, residual_in, schur, modes, coarse_inv):
    nx, ny, nz = sizes
    direct, relays = gather_plan(nz)
    sends = len(direct) + sum(len(steps) for _, steps in relays)
    plane = nx * ny
    vmem, dma = pltpu.VMEM, pltpu.SemaphoreType.DMA
    field = jax.ShapeDtypeStruct((LOADS, IF), F32)
    mult, resid = pl.pallas_call(
        functools.partial(kernel, sizes),
        out_shape=(field, field),
        in_specs=[pl.BlockSpec(memory_space=pltpu.MemorySpace.HBM)] * 4,
        out_specs=(pl.BlockSpec(memory_space=pltpu.VMEM),) * 2,
        scratch_shapes=[
            vmem((LOADS, IF), F32),
            vmem((IF, IF), F32),
            vmem((MODES, IF), F32),
            vmem((MODES, MODES * nz), F32),
            vmem((SLOT, IF), F32),
            vmem((SLOT, MODES * nz), F32),
            vmem((nz, SLOT, SLOT * nz), F32),
            vmem((SLOT * nz, SLOT * nz), BF16),
            vmem((SLOT * nz, SLOT * nz), BF16),
            vmem((6, SLOT, FACE), F32),
            vmem((IF, 256), BF16),
            vmem((AUG, IF), BF16),
            vmem((AUG, IF), BF16),
            vmem((IF, 2 * LOADS), BF16),
            vmem((2, IF, LOADS), F32),
            vmem((IF, LOADS), F32),
            vmem((IF, LOADS), F32),
            vmem((IF, LOADS), F32),
            vmem((AUG, LOADS), F32),
            vmem((IF, LOADS), F32),
            vmem((AUG, LOADS), F32),
            vmem((AUG, LOADS), F32),
            vmem((2, nz, SLOT, LOADS), F32),
            vmem((2, 4, SLOT, LOADS), F32),
            vmem((nz, SLOT, LOADS), F32),
            vmem((2, LOADS), F32),
            vmem((2, plane, 2, LOADS), F32),
            vmem((2, 6, FACE, LOADS), F32),
            dma((3,)),
            dma((6,)),
            dma((sends,)),
            dma((nz,)),
            dma((6,)),
            dma((6,)),
            dma((sends,)),
            dma((2, nz)),
            dma((6,)),
            dma((2, 6)),
            dma((4,)),
            dma((2, 4)),
            dma((plane - 1,)),
            dma((2, plane - 1)),
        ],
        compiler_params=pltpu.CompilerParams(collective_id=0, has_side_effects=True, vmem_limit_bytes=60 << 20),
    )(residual_in[0, 0, 0], schur[0, 0, 0], modes[0, 0, 0], coarse_inv[0, 0])
    return mult[None, None, None], resid[None, None, None]


def solution(mesh):
    sizes = (mesh.shape["gx"], mesh.shape["gy"], mesh.shape["gz"])
    return jax.shard_map(
        functools.partial(body, sizes),
        mesh=mesh,
        in_specs=(
            P("gx", "gy", "gz", None, None),
            P("gx", "gy", "gz", None, None),
            P("gx", "gy", "gz", None, None),
            P("gx", "gy", "gz", None),
        ),
        out_specs=(P("gx", "gy", "gz", None, None), P("gx", "gy", "gz", None, None)),
        check_vma=False,
    )
```
